32 devices in a mesh: groups: 1, seq: 32 (over z, y, x, core).
Axes of the slice: x: 2, y: 2, z: 4, core: 2. Of those that a mesh axis runs over, the one named last changes fastest.
Arguments:
- q_gate: bfloat16 [4096, 4096], P(('groups', 'seq')), may hold values from -6 to 6
- values_in: bfloat16 [4096, 4096], P(('groups', 'seq')), may hold values from -6 to 6
- decay_rate: float32 [4096, 16], replicated, as said below
- residue: float32 [4096, 16], replicated, may hold values from -3 to 3
- skip_gain: float32 [4096], replicated, may hold values from 0.5 to 1.5
- out_weight: bfloat16 [4096, 2048], P('seq'), may hold values from -0.09375 to 0.09375
Outputs:
- mixed: bfloat16 [4096, 2048], P(('groups', 'seq'))
The draws below stay inside these ranges and needn't reach their ends.
Inputs may be any that keep to these rules, and one draw needn't show every extreme that they name: `decay_rate`: every rate is positive and at most about 1/30.
All inputs are finite; a program needn't handle non-finite values.
Results may differ from the reference program's by a relative error of at most 0.0052.
Values may be sent and summed in bfloat16 or wider, within the bound.
A program may use at most 256 MiB of HBM per device.

```python
import math
import jax
import jax.numpy as jnp
from jax import lax

D = 4096
D_OUT = 2048
ORDER = 16
BLOCK = 32
TOKENS = 4096


def draw_decay_rate(key, part):
    first, second, third = jax.random.split(jax.random.fold_in(key, 11), 3)
    slow = jnp.exp(jax.random.uniform(first, (D, ORDER), jnp.float32, math.log(0.05 / TOKENS), math.log(2.0 / TOKENS)))
    fast = jnp.exp(jax.random.uniform(second, (D, ORDER), jnp.float32, math.log(1.0 / 50.0), math.log(1.0 / 30.0)))
    share_slow = 0.5
    picked = jax.random.uniform(third, (D, ORDER), jnp.float32) < share_slow
    return jnp.where(picked, slow, fast).astype(jnp.float32)


def block_scale(own_key, extent, cuts, smallest, high):
    level = 1.0
    for axis_at, blocks in cuts:
        draws = jax.random.uniform(jax.random.fold_in(jax.random.fold_in(own_key, 6), axis_at), (blocks,), jnp.float32, smallest / len(cuts), high / len(cuts))
        level = level * jnp.repeat(jnp.exp(draws), extent[axis_at] // blocks).reshape((-1,) + (1,) * (len(extent) - 1 - axis_at))
    return level


def normal_values(rng, shape, scale, bound, cuts=(), held_as=jnp.bfloat16):
    gain = block_scale(rng, shape, cuts, -0.22, 0.18) if cuts else 1.0
    result = jax.random.normal(rng, shape, jnp.float32) * scale * gain
    return jnp.minimum(jnp.maximum(result, -bound), bound).astype(held_as)


def setup_inputs(seed: int = 0, part: int = 0) -> dict:
    streams_of = jax.random.split(jax.random.key(seed), 7)
    part_splits = jax.random.split(jax.random.fold_in(streams_of[6], part), 7)
    return {
        "q_gate": normal_values(part_splits[0], (TOKENS, D), 1.0, 6.0, ((0, 32),)),
        "values_in": normal_values(part_splits[1], (TOKENS, D), 1.0, 6.0, ((0, 32),)),
        "decay_rate": draw_decay_rate(jax.random.fold_in(streams_of[6], 71), part),
        "residue": normal_values(streams_of[3], (D, ORDER), 0.5, 3.0, (), jnp.float32),
        "skip_gain": jnp.clip(jax.random.uniform(streams_of[4], (D,), jnp.float32, 0.5, 1.5), 0.5, 1.5),
        "out_weight": normal_values(streams_of[5], (D, D_OUT), D ** -0.5, 0.09375, ((0, 32),)),
    }


def gated_group(q_part, value_part, rate_part, residue_part, skip_part):
    width = q_part.shape[1]
    block_count = TOKENS // BLOCK
    rate_modes = rate_part.T
    mode_scale = jnp.sqrt(-jnp.expm1(-2.0 * rate_modes))
    mode_coef = residue_part.T * mode_scale
    position = jnp.arange(BLOCK, dtype=jnp.float32)
    tap_values = lax.optimization_barrier(jnp.sum(mode_coef[None] * jnp.exp(-position[:, None, None] * rate_modes[None]), axis=1))
    tap_round = tap_values.astype(jnp.bfloat16)
    offsets = jnp.arange(BLOCK)[:, None] - jnp.arange(BLOCK)[None, :]
    toeplitz = jnp.where((offsets >= 0)[:, :, None], tap_round[jnp.maximum(offsets, 0)], jnp.zeros((), jnp.bfloat16))
    blocked = value_part.reshape(block_count, BLOCK, width).astype(jnp.float32)
    local_part = jnp.einsum('tsg,nsg->ntg', toeplitz.astype(jnp.float32), blocked, precision=lax.Precision.HIGHEST)
    end_weight = jnp.exp(-(BLOCK - 1 - position)[:, None, None] * rate_modes[None])
    block_ends = jnp.einsum('tkg,ntg->nkg', end_weight, blocked, precision=lax.Precision.HIGHEST)
    step_decay = jnp.exp(-BLOCK * rate_modes)

    def advance(carry_state, inflow):
        return (step_decay * carry_state + inflow, carry_state)
    _, starts = lax.scan(advance, jnp.zeros((ORDER, width), jnp.float32), block_ends)
    reach_table = mode_coef[None] * jnp.exp(-(position + 1.0)[:, None, None] * rate_modes[None])
    correction = jnp.einsum('tkg,nkg->ntg', reach_table, starts, precision=lax.Precision.HIGHEST)
    conv = (local_part + correction).reshape(TOKENS, width)
    gated = q_part.astype(jnp.float32) * (conv + skip_part[None] * value_part.astype(jnp.float32))
    return gated.astype(jnp.bfloat16)

def reference(q_gate, values_in, decay_rate, residue, skip_gain, out_weight):
    group_width = min(512, D)
    group_count = D // group_width
    q_groups = q_gate.reshape(TOKENS, group_count, group_width).transpose(1, 0, 2)
    value_groups = values_in.reshape(TOKENS, group_count, group_width).transpose(1, 0, 2)
    rate_groups = decay_rate.reshape(group_count, group_width, ORDER)
    residue_groups = residue.reshape(group_count, group_width, ORDER)
    skip_groups = skip_gain.reshape(group_count, group_width)

    def one_group(inputs):
        return gated_group(inputs[0], inputs[1], inputs[2], inputs[3], inputs[4])
    gated_all = lax.map(one_group, (q_groups, value_groups, rate_groups, residue_groups, skip_groups))
    gated = gated_all.transpose(1, 0, 2).reshape(TOKENS, D)
    return jnp.dot(gated, out_weight, preferred_element_type=jnp.float32).astype(jnp.bfloat16)
```

```python
import functools

import jax
import jax.numpy as jnp
from jax import lax
from jax.experimental import pallas as pl
from jax.experimental.pallas import tpu as pltpu
from jax.sharding import PartitionSpec as P

ORDER = 16
BLOCK = 32
SUB = 8
LANES = 128
PARTS = BLOCK // SUB


def row(ref, at, lanes):
    return jnp.broadcast_to(ref[pl.ds(at, 1), lanes], (SUB, LANES))


def local_kernel(tok_rows, width, v_ref, rate_ref, res_ref, conv_ref, ends_ref, last_ref, pad, taps, mult):
    blocks = tok_rows // BLOCK
    zero = jnp.zeros((SUB, LANES), jnp.float32)
    steps = lax.broadcasted_iota(jnp.int32, (SUB, LANES), 0).astype(jnp.float32)

    def group(g, carry):
        lanes = pl.ds(pl.multiple_of(g * LANES, LANES), LANES)
        rate = rate_ref[:, lanes]
        lam = jnp.exp(-rate)
        coef = res_ref[:, lanes]
        for n in range(blocks):
            pad[n, 0:SUB, :] = zero
            pad[n, SUB : SUB + BLOCK, :] = v_ref[n * BLOCK : (n + 1) * BLOCK, lanes].astype(jnp.float32)
        for part in range(PARTS):
            mult[part * ORDER : (part + 1) * ORDER, :] = coef * jnp.exp(-float(SUB * part) * rate)
        sums = [zero] * PARTS
        for k in range(ORDER):
            base = jnp.exp(-steps * jnp.broadcast_to(rate[k : k + 1], (SUB, LANES)))
            for part in range(PARTS):
                at = part * ORDER + k
                sums[part] += base * jnp.broadcast_to(mult[at : at + 1, :], (SUB, LANES))
        for part in range(PARTS):
            taps[part * SUB : (part + 1) * SUB, :] = sums[part].astype(jnp.bfloat16).astype(jnp.float32)
        for n in range(blocks):
            acc = [zero] * PARTS
            for r in range(SUB):
                shifted = [
                    pad[n, SUB - r + SUB * i : 2 * SUB - r + SUB * i, :] for i in range(PARTS)
                ]
                for part in range(PARTS):
                    at = part * SUB + r
                    tap = jnp.broadcast_to(taps[at : at + 1, :], (SUB, LANES))
                    for i in range(part, PARTS):
                        acc[i] += tap * shifted[i - part]
            for i in range(PARTS):
                conv_ref[n * BLOCK + SUB * i : n * BLOCK + SUB * (i + 1), lanes] = acc[i]
        ends = [jnp.zeros((ORDER, LANES), jnp.float32)] * blocks
        for t in range(BLOCK):
            for n in range(blocks):
                ends[n] = lam * ends[n] + jnp.broadcast_to(pad[n, SUB + t : SUB + t + 1, :], (ORDER, LANES))
        step_decay = jnp.exp(-float(BLOCK) * rate)
        state = jnp.zeros((ORDER, LANES), jnp.float32)
        for n in range(blocks):
            ends_ref[n * ORDER : (n + 1) * ORDER, lanes] = state
            state = step_decay * state + ends[n]
        last_ref[:, lanes] = state
        return carry

    lax.fori_loop(0, width // LANES, group, 0)


def gate_kernel(tok_rows, width, q_ref, v_ref, conv_ref, ends_ref, in_ref, rate_ref, res_ref, skip_ref, out_ref, mult, whole):
    blocks = tok_rows // BLOCK
    zero = jnp.zeros((SUB, LANES), jnp.float32)
    steps = lax.broadcasted_iota(jnp.int32, (SUB, LANES), 0).astype(jnp.float32) + 1.0

    def group(g, carry):
        lanes = pl.ds(pl.multiple_of(g * LANES, LANES), LANES)
        rate = rate_ref[:, lanes]
        coef = res_ref[:, lanes]
        entering = in_ref[:, lanes]
        for n in range(blocks):
            state = ends_ref[n * ORDER : (n + 1) * ORDER, lanes] + jnp.exp(-float(BLOCK * n) * rate) * entering
            state = coef * state
            for part in range(PARTS):
                at = (n * PARTS + part) * ORDER
                mult[at : at + ORDER, :] = state * jnp.exp(-float(SUB * part) * rate)
        for k in range(ORDER):
            whole[k] = jnp.exp(-steps * jnp.broadcast_to(rate[k : k + 1], (SUB, LANES)))
        skip = jnp.broadcast_to(skip_ref[:, lanes], (BLOCK, LANES))
        for n in range(blocks):
            acc = [zero] * PARTS
            for k in range(ORDER):
                base = whole[k]
                for part in range(PARTS):
                    at = (n * PARTS + part) * ORDER + k
                    acc[part] += base * jnp.broadcast_to(mult[at : at + 1, :], (SUB, LANES))
            rows = pl.ds(n * BLOCK, BLOCK)
            conv = conv_ref[rows, lanes] + jnp.concatenate(acc, axis=0)
            value = v_ref[rows, lanes].astype(jnp.float32)
            gated = q_ref[rows, lanes].astype(jnp.float32) * (conv + skip * value)
            out_ref[rows, lanes] = gated.astype(jnp.bfloat16)
        return carry

    lax.fori_loop(0, width // LANES, group, 0)


def scan_kernel(count, tok_rows, in_ref, rate_ref, out_ref):
    decay = jnp.exp(-float(tok_rows) * rate_ref[...])

    def hop(i, state):
        out_ref[i] = state
        return decay * state + in_ref[i]

    lax.fori_loop(0, count, hop, jnp.zeros_like(decay))


def on_device(q_gate, values_in, decay_rate, residue, skip_gain, out_weight):
    tok_rows, width = q_gate.shape
    out_width = out_weight.shape[1]
    half = out_width // 2
    count = lax.axis_size("seq")
    me = lax.axis_index("seq")
    core = me % 2
    swap = [(i, i ^ 1) for i in range(count)]

    keep = lax.dynamic_slice_in_dim(out_weight, core * half, half, 1)
    give = lax.dynamic_slice_in_dim(out_weight, (1 - core) * half, half, 1)
    take = lax.ppermute(give, "seq", swap)
    pair = jnp.where(core == 0, jnp.concatenate([keep, take]), jnp.concatenate([take, keep]))
    sides = [list(range(0, count, 2)), list(range(1, count, 2))]
    weights = lax.all_gather(pair, "seq", axis=0, tiled=True, axis_index_groups=sides)

    rate = decay_rate.T
    coef = residue.T * jnp.sqrt(-jnp.expm1(-2.0 * rate))
    chunk = 1024
    blocks = tok_rows // BLOCK
    grid = (width // chunk,)
    tall = lambda rows: pl.BlockSpec((rows, chunk), lambda c: (0, c))
    conv, starts, last = pl.pallas_call(
        functools.partial(local_kernel, tok_rows, chunk),
        grid=grid,
        in_specs=[tall(tok_rows), tall(ORDER), tall(ORDER)],
        out_specs=[tall(tok_rows), tall(blocks * ORDER), tall(ORDER)],
        out_shape=[
            jax.ShapeDtypeStruct((tok_rows, width), jnp.float32),
            jax.ShapeDtypeStruct((blocks * ORDER, width), jnp.float32),
            jax.ShapeDtypeStruct((ORDER, width), jnp.float32),
        ],
        scratch_shapes=[
            pltpu.VMEM((blocks, SUB + BLOCK, LANES), jnp.float32),
            pltpu.VMEM((BLOCK, LANES), jnp.float32),
            pltpu.VMEM((PARTS * ORDER, LANES), jnp.float32),
        ],
        name="local_conv",
    )(values_in, rate, coef)

    own = width // count
    spread = last.reshape(ORDER, count, own).transpose(1, 0, 2)
    owned = lax.all_to_all(spread, "seq", 0, 0, tiled=True)
    rate_own = lax.dynamic_slice_in_dim(rate, me * own, own, 1)
    scanned = pl.pallas_call(
        functools.partial(scan_kernel, count, tok_rows),
        out_shape=jax.ShapeDtypeStruct((count, ORDER, own), jnp.float32),
        name="state_scan",
    )(owned, rate_own)
    back = lax.all_to_all(scanned, "seq", 0, 0, tiled=True)
    entering = back.transpose(1, 0, 2).reshape(ORDER, width)

    gated = pl.pallas_call(
        functools.partial(gate_kernel, tok_rows, chunk),
        grid=grid,
        in_specs=[tall(tok_rows), tall(tok_rows), tall(tok_rows), tall(blocks * ORDER), tall(ORDER), tall(ORDER), tall(ORDER), tall(1)],
        out_specs=tall(tok_rows),
        out_shape=jax.ShapeDtypeStruct((tok_rows, width), jnp.bfloat16),
        scratch_shapes=[
            pltpu.VMEM((blocks * PARTS * ORDER, LANES), jnp.float32),
            pltpu.VMEM((ORDER, SUB, LANES), jnp.float32),
        ],
        name="gate",
    )(q_gate, values_in, conv, starts, entering, rate, coef, skip_gain[None])

    other = lax.ppermute(gated, "seq", swap)
    both = jnp.concatenate([gated, other])
    mixed = jnp.dot(both, weights, preferred_element_type=jnp.float32).astype(jnp.bfloat16)
    mine = mixed[:tok_rows]
    far = lax.ppermute(mixed[tok_rows:], "seq", swap)
    return jnp.where(core == 0, jnp.concatenate([mine, far], 1), jnp.concatenate([far, mine], 1))


def solution(mesh):
    in_specs = (
        P(("groups", "seq"), None),
        P(("groups", "seq"), None),
        P(),
        P(),
        P(),
        P("seq", None),
    )
    out_specs = P(("groups", "seq"), None)
    return jax.shard_map(
        on_device, mesh=mesh, in_specs=in_specs, out_specs=out_specs, check_vma=False
    )
```

```python
import functools
import math

import jax
import jax.numpy as jnp
from jax import lax
from jax.experimental import pallas as pl
from jax.experimental.pallas import tpu as pltpu
from jax.sharding import PartitionSpec as P

ORDER = 16
BLOCK = 32
SUB = 8
LANES = 128
PARTS = BLOCK // SUB
GRID = (4, 2, 2)
MESH = pl.DeviceIdType.MESH


def row(ref, at, lanes):
    return jnp.broadcast_to(ref[pl.ds(at, 1), lanes], (SUB, LANES))


def local_group(tok_rows, v_ref, rate_ref, res_ref, conv_ref, ends_ref, put_last, pad, taps, mult):
    blocks = tok_rows // BLOCK
    zero = jnp.zeros((SUB, LANES), jnp.float32)
    steps = lax.broadcasted_iota(jnp.int32, (SUB, LANES), 0).astype(jnp.float32)

    def group(g, carry):
        lanes = pl.ds(pl.multiple_of(g * LANES, LANES), LANES)
        rate = rate_ref[:, lanes]
        lam = jnp.exp(-rate)
        coef = res_ref[:, lanes]
        for n in range(blocks):
            pad[n, 0:SUB, :] = zero
            pad[n, SUB : SUB + BLOCK, :] = v_ref[n * BLOCK : (n + 1) * BLOCK, lanes].astype(jnp.float32)
        for part in range(PARTS):
            mult[part * ORDER : (part + 1) * ORDER, :] = coef * jnp.exp(-float(SUB * part) * rate)
        sums = [zero] * PARTS
        for k in range(ORDER):
            base = jnp.exp(-steps * jnp.broadcast_to(rate[k : k + 1], (SUB, LANES)))
            for part in range(PARTS):
                at = part * ORDER + k
                sums[part] += base * jnp.broadcast_to(mult[at : at + 1, :], (SUB, LANES))
        for part in range(PARTS):
            taps[part * SUB : (part + 1) * SUB, :] = sums[part].astype(jnp.bfloat16).astype(jnp.float32)
        for n in range(blocks):
            acc = [zero] * PARTS
            for r in range(SUB):
                shifted = [
                    pad[n, SUB - r + SUB * i : 2 * SUB - r + SUB * i, :] for i in range(PARTS)
                ]
                for part in range(PARTS):
                    at = part * SUB + r
                    tap = jnp.broadcast_to(taps[at : at + 1, :], (SUB, LANES))
                    for i in range(part, PARTS):
                        acc[i] += tap * shifted[i - part]
            for i in range(PARTS):
                conv_ref[n * BLOCK + SUB * i : n * BLOCK + SUB * (i + 1), lanes] = acc[i]
        ends = [jnp.zeros((ORDER, LANES), jnp.float32)] * blocks
        for t in range(BLOCK):
            for n in range(blocks):
                ends[n] = lam * ends[n] + jnp.broadcast_to(pad[n, SUB + t : SUB + t + 1, :], (ORDER, LANES))
        step_decay = jnp.exp(-float(BLOCK) * rate)
        state = jnp.zeros((ORDER, LANES), jnp.float32)
        for n in range(blocks):
            ends_ref[n * ORDER : (n + 1) * ORDER, lanes] = state
            state = step_decay * state + ends[n]
        put_last(g, lanes, state)
        return carry

    return group


def local_kernel(tok_rows, width, v_ref, rate_ref, res_ref, conv_ref, ends_ref, last_ref, pad, taps, mult):
    def put_last(g, lanes, state):
        last_ref[:, lanes] = state

    group = local_group(tok_rows, v_ref, rate_ref, res_ref, conv_ref, ends_ref, put_last, pad, taps, mult)
    lax.fori_loop(0, width // LANES, group, 0)


def gate_group(tok_rows, q_ref, v_ref, conv_ref, ends_ref, get_state, rate_ref, res_ref, skip_ref, out_ref, mult, whole):
    blocks = tok_rows // BLOCK
    zero = jnp.zeros((SUB, LANES), jnp.float32)
    steps = lax.broadcasted_iota(jnp.int32, (SUB, LANES), 0).astype(jnp.float32) + 1.0

    def group(g, carry):
        lanes = pl.ds(pl.multiple_of(g * LANES, LANES), LANES)
        rate = rate_ref[:, lanes]
        coef = res_ref[:, lanes]
        entering = get_state(g, lanes)
        for n in range(blocks):
            state = ends_ref[n * ORDER : (n + 1) * ORDER, lanes] + jnp.exp(-float(BLOCK * n) * rate) * entering
            state = coef * state
            for part in range(PARTS):
                at = (n * PARTS + part) * ORDER
                mult[at : at + ORDER, :] = state * jnp.exp(-float(SUB * part) * rate)
        for k in range(ORDER):
            whole[k] = jnp.exp(-steps * jnp.broadcast_to(rate[k : k + 1], (SUB, LANES)))
        skip = jnp.broadcast_to(skip_ref[:, lanes], (BLOCK, LANES))
        for n in range(blocks):
            acc = [zero] * PARTS
            for k in range(ORDER):
                base = whole[k]
                for part in range(PARTS):
                    at = (n * PARTS + part) * ORDER + k
                    acc[part] += base * jnp.broadcast_to(mult[at : at + 1, :], (SUB, LANES))
            rows = pl.ds(n * BLOCK, BLOCK)
            conv = conv_ref[rows, lanes] + jnp.concatenate(acc, axis=0)
            value = v_ref[rows, lanes].astype(jnp.float32)
            gated = q_ref[rows, lanes].astype(jnp.float32) * (conv + skip * value)
            out_ref[rows, lanes] = gated.astype(jnp.bfloat16)
        return carry

    return group


def gate_kernel(tok_rows, width, q_ref, v_ref, conv_ref, ends_ref, in_ref, rate_ref, res_ref, skip_ref, out_ref, mult, whole):
    group = gate_group(
        tok_rows, q_ref, v_ref, conv_ref, ends_ref, lambda g, lanes: in_ref[:, lanes], rate_ref, res_ref, skip_ref, out_ref, mult, whole
    )
    lax.fori_loop(0, width // LANES, group, 0)


def scan_kernel(count, tok_rows, in_ref, rate_ref, out_ref):
    decay = jnp.exp(-float(tok_rows) * rate_ref[...])

    def hop(i, state):
        out_ref[i] = state
        return decay * state + in_ref[i]

    lax.fori_loop(0, count, hop, jnp.zeros_like(decay))


def layer_kernel(
    tok_rows, width, out_width, count,
    q_ref, v_ref, rate_ref, res_ref, skip_ref, ow_ref, out_ref,
    conv, ends, gated, other, last, owned, scanned, back, keeps, takes, total, theirs, far,
    pad, taps, mult_a, mult_b, whole,
    w_send, w_recv, a_send, a_recv, b_send, b_recv, p_send, p_recv,
):
    zs, ys, xs = GRID
    half = out_width // 2
    own = width // count
    groups = width // LANES
    me = lax.axis_index("seq")
    core, x, y, z = me % 2, (me // 2) % xs, (me // (2 * xs)) % ys, me // (2 * xs * ys)
    place = lambda z, y, x: ((z * ys + y) * xs + x) * 2 + core
    up, flip_y, flip_x = place((z + 1) % zs, y, x), place(z, 1 - y, x), place(z, y, 1 - x)
    partner = me + 1 - 2 * core
    mine_cols = pl.ds(pl.multiple_of(core * half, LANES), half)
    other_cols = pl.ds(pl.multiple_of((1 - core) * half, LANES), half)

    barrier = pltpu.get_barrier_semaphore()

    def greet(d, carry):
        pl.semaphore_signal(barrier, inc=1, device_id={"seq": (me + d) % count}, device_id_type=MESH)
        return carry

    lax.fori_loop(1, count, greet, 0)
    pl.semaphore_wait(barrier, count - 1)

    slot = lambda at: (at[0] * ys + at[1]) * xs + at[2]
    copies = {}

    def send(kind, at, to, device):
        buffer = keeps if kind == "k" else takes
        source = ow_ref.at[:, mine_cols] if kind == "k" and slot(at) == 0 else buffer.at[slot(at)]
        number = len(copies)
        copy = pltpu.make_async_remote_copy(
            src_ref=source, dst_ref=buffer.at[slot(to)], send_sem=w_send.at[number], recv_sem=w_recv.at[number],
            device_id={"seq": device}, device_id_type=MESH,
        )
        copy.start()
        copies[kind, to] = copy

    def arrived(kind, at):
        copies[kind, at].wait_recv()

    def first(kind, dz):
        if kind == "k":
            send("k", (dz, 0, 0), (dz, 0, 1), flip_x)
            send("k", (dz, 0, 0), (dz, 1, 0), flip_y)
        else:
            send("t", (dz, 0, 0), (dz, 1, 0), flip_y)
            send("t", (dz, 0, 0), (dz, 0, 1), flip_x)
        if dz + 1 < zs:
            send(kind, (dz, 0, 0), (dz + 1, 0, 0), up)

    def second(dz):
        arrived("k", (dz, 0, 1))
        send("k", (dz, 0, 1), (dz, 1, 1), flip_y)
        arrived("t", (dz, 1, 0))
        send("t", (dz, 1, 0), (dz, 1, 1), flip_x)

    def round_of(dz):
        for kind in "kt":
            arrived(kind, (dz, 0, 0))
            first(kind, dz)
        second(dz - 1)

    swap_w = pltpu.make_async_remote_copy(
        src_ref=ow_ref.at[:, other_cols], dst_ref=takes.at[0], send_sem=p_send.at[0], recv_sem=p_recv.at[0],
        device_id={"seq": partner}, device_id_type=MESH,
    )
    swap_w.start()
    first("k", 0)

    def put_last(g, lanes, state):
        last[g] = state

    conv_group = local_group(tok_rows, v_ref, rate_ref, res_ref, conv, ends, put_last, pad, taps, mult_a)
    lax.fori_loop(0, groups // 8, conv_group, 0)
    swap_w.wait_recv()
    first("t", 0)
    lax.fori_loop(groups // 8, groups, conv_group, 0)

    def exchange(source, target, ssem, rsem):
        def one(d):
            return pltpu.make_async_remote_copy(
                src_ref=source.at[(me + d) % count], dst_ref=target.at[me], send_sem=ssem.at[d], recv_sem=rsem.at[d],
                device_id={"seq": (me + d) % count}, device_id_type=MESH,
            )

        def from_there(d):
            return pltpu.make_async_remote_copy(
                src_ref=source.at[(me + d) % count], dst_ref=target.at[(me + count - d) % count],
                send_sem=ssem.at[d], recv_sem=rsem.at[d],
                device_id={"seq": (me + d) % count}, device_id_type=MESH,
            )

        def start(d, carry):
            one(d).start()
            return carry

        def finish(d, carry):
            from_there(d).wait_recv()
            return carry

        def sent(d, carry):
            one(d).wait_send()
            return carry

        lax.fori_loop(1, count, start, 0)
        return lambda: lax.fori_loop(1, count, finish, 0), lambda: lax.fori_loop(1, count, sent, 0)

    ready_a, sent_a = exchange(last, owned, a_send, a_recv)
    owned[me] = last[me]
    round_of(1)
    ready_a()
    decay = jnp.exp(-float(tok_rows) * rate_ref[:, pl.ds(pl.multiple_of(me * own, LANES), own)])

    def hop(i, state):
        scanned[i] = state
        return decay * state + owned[i]

    lax.fori_loop(0, count, hop, jnp.zeros_like(decay))
    ready_b, sent_b = exchange(scanned, back, b_send, b_recv)
    back[me] = scanned[me]
    round_of(2)
    ready_b()
    gate = gate_group(
        tok_rows, q_ref, v_ref, conv, ends, lambda g, lanes: back[g], rate_ref, res_ref, skip_ref, gated, mult_b, whole
    )
    lax.fori_loop(0, groups, gate, 0)
    swap_g = pltpu.make_async_remote_copy(
        src_ref=gated, dst_ref=other, send_sem=p_send.at[1], recv_sem=p_recv.at[1],
        device_id={"seq": partner}, device_id_type=MESH,
    )
    swap_g.start()
    round_of(3)
    second(3)
    swap_g.wait_recv()

    tile = 256

    def multiply(dz):
        for dy in range(ys):
            for dx in range(xs):
                at = (dz, dy, dx)
                chip = (((z + zs - dz) % zs) * ys + (y + dy) % ys) * xs + (x + dx) % xs
                near = pl.ds(pl.multiple_of((2 * chip + core) * own, LANES), own)
                away = pl.ds(pl.multiple_of((2 * chip + 1 - core) * own, LANES), own)
                left = jnp.concatenate(
                    [
                        jnp.concatenate([gated[:, near], gated[:, away]], axis=1),
                        jnp.concatenate([other[:, near], other[:, away]], axis=1),
                    ],
                    axis=0,
                )

                def column(n, carry):
                    cols = pl.ds(pl.multiple_of(n * tile, LANES), tile)
                    if slot(at) == 0:
                        kept = ow_ref[:, pl.ds(pl.multiple_of(core * half + n * tile, LANES), tile)]
                    else:
                        kept = keeps[slot(at), :, cols]
                    right = jnp.concatenate([kept, takes[slot(at), :, cols]], axis=0)
                    term = jnp.dot(left, right, preferred_element_type=jnp.float32)
                    if slot(at) == 0:
                        total[:, cols] = term
                    else:
                        total[:, cols] += term
                    return carry

                lax.fori_loop(0, half // tile, column, 0)

    for dz in range(zs):
        for kind, at in (("k", (dz, 1, 0)), ("t", (dz, 0, 1)), ("k", (dz, 1, 1)), ("t", (dz, 1, 1))):
            arrived(kind, at)
        multiply(dz)

    theirs[...] = total[tok_rows:, :].astype(jnp.bfloat16)
    swap_o = pltpu.make_async_remote_copy(
        src_ref=theirs, dst_ref=far, send_sem=p_send.at[2], recv_sem=p_recv.at[2],
        device_id={"seq": partner}, device_id_type=MESH,
    )
    swap_o.start()
    out_ref[:, mine_cols] = total[:tok_rows, :].astype(jnp.bfloat16)
    swap_w.wait_send()
    swap_g.wait_send()
    for copy in copies.values():
        copy.wait_send()
    sent_a()
    sent_b()
    swap_o.wait()
    out_ref[:, other_cols] = far[...]


def layer(q_gate, values_in, rate, coef, skip, out_weight, count):
    tok_rows, width = q_gate.shape
    out_width = out_weight.shape[1]
    half = out_width // 2
    blocks = tok_rows // BLOCK
    chips = math.prod(GRID)
    states = pltpu.VMEM((count, ORDER, width // count), jnp.float32)
    weights = pltpu.VMEM((chips, out_weight.shape[0], half), jnp.bfloat16)
    copies = 2 * (chips - 1)
    dma = lambda n: pltpu.SemaphoreType.DMA((n,))
    return pl.pallas_call(
        functools.partial(layer_kernel, tok_rows, width, out_width, count),
        in_specs=[pl.BlockSpec(memory_space=pltpu.VMEM)] * 6,
        out_specs=pl.BlockSpec(memory_space=pltpu.VMEM),
        out_shape=jax.ShapeDtypeStruct((tok_rows, out_width), jnp.bfloat16),
        scratch_shapes=[
            pltpu.VMEM((tok_rows, width), jnp.float32),
            pltpu.VMEM((blocks * ORDER, width), jnp.float32),
            pltpu.VMEM((tok_rows, width), jnp.bfloat16),
            pltpu.VMEM((tok_rows, width), jnp.bfloat16),
            states, states, states, states,
            weights, weights,
            pltpu.VMEM((2 * tok_rows, half), jnp.float32),
            pltpu.VMEM((tok_rows, half), jnp.bfloat16),
            pltpu.VMEM((tok_rows, half), jnp.bfloat16),
            pltpu.VMEM((blocks, SUB + BLOCK, LANES), jnp.float32),
            pltpu.VMEM((BLOCK, LANES), jnp.float32),
            pltpu.VMEM((PARTS * ORDER, LANES), jnp.float32),
            pltpu.VMEM((blocks * PARTS * ORDER, LANES), jnp.float32),
            pltpu.VMEM((ORDER, SUB, LANES), jnp.float32),
            dma(copies), dma(copies), dma(count), dma(count), dma(count), dma(count), dma(3), dma(3),
        ],
        compiler_params=pltpu.CompilerParams(collective_id=0, has_side_effects=True),
        name="layer",
    )(q_gate, values_in, rate, coef, skip, out_weight)


def on_device(q_gate, values_in, decay_rate, residue, skip_gain, out_weight):
    tok_rows, width = q_gate.shape
    out_width = out_weight.shape[1]
    half = out_width // 2
    count = lax.axis_size("seq")
    me = lax.axis_index("seq")
    core = me % 2
    swap = [(i, i ^ 1) for i in range(count)]

    rate = decay_rate.T
    coef = residue.T * jnp.sqrt(-jnp.expm1(-2.0 * rate))
    if count == 2 * math.prod(GRID) and width == count * LANES:
        return layer(q_gate, values_in, rate, coef, skip_gain[None], out_weight, count)

    keep = lax.dynamic_slice_in_dim(out_weight, core * half, half, 1)
    give = lax.dynamic_slice_in_dim(out_weight, (1 - core) * half, half, 1)
    take = lax.ppermute(give, "seq", swap)
    pair = jnp.where(core == 0, jnp.concatenate([keep, take]), jnp.concatenate([take, keep]))
    sides = [list(range(0, count, 2)), list(range(1, count, 2))]
    weights = lax.all_gather(pair, "seq", axis=0, tiled=True, axis_index_groups=sides)

    chunk = 1024
    blocks = tok_rows // BLOCK
    grid = (width // chunk,)
    tall = lambda rows: pl.BlockSpec((rows, chunk), lambda c: (0, c))
    conv, starts, last = pl.pallas_call(
        functools.partial(local_kernel, tok_rows, chunk),
        grid=grid,
        in_specs=[tall(tok_rows), tall(ORDER), tall(ORDER)],
        out_specs=[tall(tok_rows), tall(blocks * ORDER), tall(ORDER)],
        out_shape=[
            jax.ShapeDtypeStruct((tok_rows, width), jnp.float32),
            jax.ShapeDtypeStruct((blocks * ORDER, width), jnp.float32),
            jax.ShapeDtypeStruct((ORDER, width), jnp.float32),
        ],
        scratch_shapes=[
            pltpu.VMEM((blocks, SUB + BLOCK, LANES), jnp.float32),
            pltpu.VMEM((BLOCK, LANES), jnp.float32),
            pltpu.VMEM((PARTS * ORDER, LANES), jnp.float32),
        ],
        name="local_conv",
    )(values_in, rate, coef)

    own = width // count
    spread = last.reshape(ORDER, count, own).transpose(1, 0, 2)
    owned = lax.all_to_all(spread, "seq", 0, 0, tiled=True)
    rate_own = lax.dynamic_slice_in_dim(rate, me * own, own, 1)
    scanned = pl.pallas_call(
        functools.partial(scan_kernel, count, tok_rows),
        out_shape=jax.ShapeDtypeStruct((count, ORDER, own), jnp.float32),
        name="state_scan",
    )(owned, rate_own)
    back = lax.all_to_all(scanned, "seq", 0, 0, tiled=True)
    entering = back.transpose(1, 0, 2).reshape(ORDER, width)

    gated = pl.pallas_call(
        functools.partial(gate_kernel, tok_rows, chunk),
        grid=grid,
        in_specs=[tall(tok_rows), tall(tok_rows), tall(tok_rows), tall(blocks * ORDER), tall(ORDER), tall(ORDER), tall(ORDER), tall(1)],
        out_specs=tall(tok_rows),
        out_shape=jax.ShapeDtypeStruct((tok_rows, width), jnp.bfloat16),
        scratch_shapes=[
            pltpu.VMEM((blocks * PARTS * ORDER, LANES), jnp.float32),
            pltpu.VMEM((ORDER, SUB, LANES), jnp.float32),
        ],
        name="gate",
    )(q_gate, values_in, conv, starts, entering, rate, coef, skip_gain[None])

    other = lax.ppermute(gated, "seq", swap)
    both = jnp.concatenate([gated, other])
    mixed = jnp.dot(both, weights, preferred_element_type=jnp.float32).astype(jnp.bfloat16)
    mine = mixed[:tok_rows]
    far = lax.ppermute(mixed[tok_rows:], "seq", swap)
    return jnp.where(core == 0, jnp.concatenate([mine, far], 1), jnp.concatenate([far, mine], 1))


def solution(mesh):
    in_specs = (
        P(("groups", "seq"), None),
        P(("groups", "seq"), None),
        P(),
        P(),
        P(),
        P("seq", None),
    )
    out_specs = P(("groups", "seq"), None)
    return jax.shard_map(
        on_device, mesh=mesh, in_specs=in_specs, out_specs=out_specs, check_vma=False
    )
```
